256 devices in a mesh: ctx: 64 (over x, z, core), tp: 4 (over y).
Axes of the slice: x: 4, y: 4, z: 8, core: 2. Of those that a mesh axis runs over, the one named last changes fastest.
Arguments:
- streams: bfloat16 [10240, 3, 4096], P('ctx', None, 'tp'), may hold values from -6 to 6
- short_taps: float32 [7, 3, 4096], P(None, None, 'tp'), may hold values from -2 to 2
- mix_taps: float32 [128, 4096], P(None, 'tp'), may hold values from -0.5 to 0.5
- pole_rate: float32 [16, 4096], P(None, 'tp'), may hold values from 9.765625e-06 to 0.06, as said below
- pole_angle: float32 [16, 4096], P(None, 'tp'), may hold values from -3.140625 to 3.140625
- residue: float32 [2, 16, 4096], P(None, None, 'tp'), may hold values from -1.5 to 1.5
- skip: float32 [4096], P('tp'), may hold values from -3 to 3
- out_weight: bfloat16 [4096, 4096], P('tp', 'ctx'), may hold values from -0.25 to 0.25
Outputs:
- mixed: bfloat16 [10240, 4096], P('ctx', 'tp')
The draws below stay inside these ranges and needn't reach their ends.
Inputs may be any that keep to these rules, and one draw needn't show every extreme that they name: `pole_rate`: each pole's decay rate is positive.
All inputs are finite; a program needn't handle non-finite values.
Results may differ from the reference program's by a relative error of at most 0.0057.
Values may be sent and summed in bfloat16 or wider, within the bound.
A program may use at most 64 MiB of HBM per device.

```python
import math
import jax
import jax.numpy as jnp
from jax import lax

D = 4096
DOUT = 4096
MODES = 16
TOK_DEV = 160
TOKENS = 10240
N_CTX = 64


def draw_pole_rate(key, part):
    key_pick, key_slow, key_fast = jax.random.split(key, 3)
    share = 0.5
    pick = jax.random.uniform(key_pick, (MODES, D)) < share
    slow = jnp.exp(jax.random.uniform(key_slow, (MODES, D), minval=math.log(0.05), maxval=0.0)) * (2.3 / TOKENS)
    fast = jnp.exp(jax.random.uniform(key_fast, (MODES, D), minval=math.log(0.025), maxval=math.log(0.06)))
    return jnp.where(pick, slow, fast).astype(jnp.float32)


def strengthened(result, own_key, source, target, shards_of, factor):
    def block_of(axis_at):
        return (jnp.arange(result.shape[axis_at]) // (result.shape[axis_at] // shards_of)).reshape((-1,) + (1,) * (result.ndim - 1 - axis_at))

    near = jax.random.permutation(own_key, shards_of)[block_of(target)]
    other_side = (block_of(target) + shards_of // 2) % shards_of
    return jnp.where((block_of(source) == near) | (block_of(source) == other_side), factor * result, result)


def level_of(own_key, extent, cuts, low, top_value):
    def one(position, parts):
        heights = jax.random.uniform(jax.random.fold_in(jax.random.fold_in(own_key, 6), position), (parts,), jnp.float32, low / len(cuts), top_value / len(cuts))
        return jnp.repeat(jnp.exp(heights), extent[position] // parts).reshape((-1,) + (1,) * (len(extent) - position - 1))

    loudness = one(*cuts[0])
    for cut in cuts[1:]:
        loudness = loudness * one(*cut)
    return loudness


def bell_draw(stream_key, shape, spread, reach, cuts=(), kind=jnp.bfloat16):
    result = spread * jax.random.normal(stream_key, shape, jnp.float32)
    if cuts:
        result = result * level_of(stream_key, shape, cuts, -0.22, 0.18)
    return jnp.clip(result, -reach, reach).astype(kind)


def heavy_noise(key, extent, spread, reach, cuts, heavy, kind=jnp.bfloat16):
    result = spread * jax.random.normal(key, extent, jnp.float32)
    if cuts:
        result = result * level_of(key, extent, cuts, -0.22, 0.18)
    return jnp.clip(strengthened(result, jax.random.fold_in(key, 3), *heavy), -reach, reach).astype(kind)


def setup_inputs(seed: int = 0) -> dict:
    key_of = jax.random.split(jax.random.key(seed), 9)
    streams = bell_draw(key_of[0], (TOKENS, 3, D), 1.0, 6.0, ((0, 64), (2, 4)))
    short_taps = bell_draw(key_of[1], (7, 3, D), 7 ** -0.5, 2.0, ((2, 4),), jnp.float32)
    mix_taps = bell_draw(key_of[2], (128, D), 128 ** -0.5, 0.5, ((1, 4),), jnp.float32)
    pole_rate = draw_pole_rate(jax.random.fold_in(key_of[8], 71), 0)
    pole_angle = jnp.clip(jax.random.uniform(key_of[4], (MODES, D), jnp.float32, -3.140625, 3.140625), -3.140625, 3.140625)
    residue = bell_draw(key_of[5], (2, MODES, D), 0.25, 1.5, ((2, 4),), jnp.float32)
    skip = bell_draw(key_of[6], (D,), 0.5, 3.0, ((0, 4),), jnp.float32)
    out_weight = heavy_noise(key_of[7], (D, DOUT), D ** -0.5, 0.25, ((0, 4), (1, 64)), (0, 1, 64, 4.0))
    return {"streams": streams, "short_taps": short_taps, "mix_taps": mix_taps, "pole_rate": pole_rate, "pole_angle": pole_angle, "residue": residue, "skip": skip, "out_weight": out_weight}


def fft_causal(ext, taps, rows):
    width = taps.shape[0]
    total = ext.shape[0] + width
    spec = jnp.fft.rfft(ext, n=total, axis=0) * jnp.fft.rfft(taps, n=total, axis=0)
    full = jnp.fft.irfft(spec, n=total, axis=0)
    start = ext.shape[0] - rows
    return full[start:start + rows].astype(jnp.float32)

def reference(streams, short_taps, mix_taps, pole_rate, pole_angle, residue, skip, out_weight):
    rows = TOK_DEV
    blocks = streams.reshape(N_CTX, rows, 3, D)
    amp = jnp.sqrt(1.0 - jnp.exp(-2.0 * pole_rate))
    res_re = residue[0] * amp
    res_im = residue[1] * amp
    dec_mag = jnp.exp(-pole_rate * rows)
    dec_re = dec_mag * jnp.cos(pole_angle * rows)
    dec_im = dec_mag * jnp.sin(pole_angle * rows)
    steps = jnp.arange(rows).astype(jnp.float32)[:, None]

    def one_block(carry, block):
        rim, st_re, st_im = carry
        ext = jnp.concatenate([rim, block], 0).astype(jnp.float32)
        span = rows + 127
        short = jnp.zeros((span, 3, D), jnp.float32)
        for lag in range(7):
            short = short + short_taps[lag][None] * ext[6 - lag:6 - lag + span]
        gate = (short[:, 1] * short[:, 2]).astype(jnp.bfloat16)
        query = short[127:, 0]
        medium = fft_causal(gate.astype(jnp.float32), mix_taps, rows)
        filt = jnp.zeros((rows, D), jnp.float32)
        inflow = jnp.zeros((rows, D), jnp.float32)
        flipped = medium[::-1]
        end_re = []
        end_im = []
        for mode in range(MODES):
            mag = jnp.exp(-pole_rate[mode][None] * steps)
            cosk = mag * jnp.cos(pole_angle[mode][None] * steps)
            sink = mag * jnp.sin(pole_angle[mode][None] * steps)
            filt = filt + res_re[mode][None] * cosk - res_im[mode][None] * sink
            end_re.append(lax.optimization_barrier(jnp.sum(flipped * cosk, 0)))
            end_im.append(lax.optimization_barrier(jnp.sum(flipped * sink, 0)))
            later = steps + 1.0
            mag1 = jnp.exp(-pole_rate[mode][None] * later)
            cos1 = mag1 * jnp.cos(pole_angle[mode][None] * later)
            sin1 = mag1 * jnp.sin(pole_angle[mode][None] * later)
            are = res_re[mode] * st_re[mode] - res_im[mode] * st_im[mode]
            aim = res_re[mode] * st_im[mode] + res_im[mode] * st_re[mode]
            inflow = inflow + are[None] * cos1 - aim[None] * sin1
        intra = fft_causal(medium, filt, rows)
        longf = intra + inflow + skip[None] * medium
        hidden = (query * longf).astype(jnp.bfloat16)
        out = jnp.dot(hidden, out_weight, preferred_element_type=jnp.float32).astype(jnp.bfloat16)
        e_re = jnp.stack(end_re, 0)
        e_im = jnp.stack(end_im, 0)
        new_re = dec_re * st_re - dec_im * st_im + e_re
        new_im = dec_re * st_im + dec_im * st_re + e_im
        return ((block[rows - 133:], new_re, new_im), out)
    init = (jnp.zeros((133, 3, D), jnp.bfloat16), jnp.zeros((MODES, D), jnp.float32), jnp.zeros((MODES, D), jnp.float32))
    final, outs = lax.scan(one_block, init, blocks)
    return outs.reshape(TOKENS, DOUT)
```

```python
import functools

import jax
import jax.numpy as jnp
from jax import lax
from jax.experimental import pallas as pl
from jax.experimental.pallas import tpu as pltpu
from jax.sharding import PartitionSpec as P

MESH = pl.DeviceIdType.MESH
SUB = 8
HALO = 128
XH = 8
GROUP = 4
F32 = jnp.float32
BF16 = jnp.bfloat16


def mixer_kernel(
    n,
    x_ref,
    staps_ref,
    mtaps_ref,
    rate_ref,
    angle_ref,
    res_ref,
    skip_ref,
    hid_ref,
    xf,
    gext,
    gsend,
    ghalo,
    tail,
    qs,
    med,
    loc,
    hid32,
    xr,
    xi,
    qr,
    qi,
    pr_s,
    pi_s,
    a1_s,
    a2_s,
    rr_s,
    ri_s,
    b1_s,
    p20r,
    p20i,
    p40r,
    p40i,
    p80r,
    p80i,
    p160r,
    p160i,
    mt_s,
    ebuf,
    rbuf,
    obuf,
    sbuf,
    halo_send,
    halo_recv,
    s1,
    r1,
    s2,
    r2,
):
    rows, width = hid_ref.shape
    span = rows // SUB
    modes = rate_ref.shape[0]
    groups = modes // GROUP
    tiles = width // 128
    total = groups * tiles
    stride = n // total
    me = lax.axis_index("ctx")
    nxt = lax.rem(me + 1, n)

    def lanes(l):
        return pl.ds(pl.multiple_of(l * 128, 128), 128)

    def fixed_row(ref, r, l):
        return jnp.broadcast_to(ref[pl.ds(r, 1), lanes(l)], (SUB, 128))

    def row(ref, r, l):
        return ref[l, pl.ds(r, SUB, stride=0), :]

    def put(ref, value):
        for t in range(tiles):
            ref[t] = value[:, t * 128 : (t + 1) * 128]

    barrier = pltpu.get_barrier_semaphore()

    def greet(r, c):
        pl.semaphore_signal(
            barrier, inc=1, device_id={"ctx": lax.rem(me + r, n)}, device_id_type=MESH
        )
        return c

    lax.fori_loop(1, n, greet, 0)

    for t in range(tiles):
        mt_s[t] = mtaps_ref[:, pl.ds(t * 128, 128)]

    for s in range(3):
        for t in range(tiles):
            xf[s * tiles + t, pl.ds(0, XH), :] = jnp.zeros((XH, 128), F32)

        def widen(i, c, s=s):
            at = pl.multiple_of(i * 16, 16)
            to = pl.multiple_of(XH + i * 16, 8)
            block = x_ref[s, pl.ds(at, 16), :].astype(F32)
            for t in range(tiles):
                xf[s * tiles + t, pl.ds(to, 16), :] = block[:, t * 128 : (t + 1) * 128]
            return c

        lax.fori_loop(0, rows // 16, widen, 0)

    def short(s, l, first, last):
        taps = [fixed_row(staps_ref, s * 8 + j, l) for j in range(7)]
        got = {}
        for d in range(first - 6, last):
            got[d] = xf[s * tiles + l, pl.ds(XH + d, SUB, stride=span), :]
        out = []
        for k in range(first, last):
            acc = taps[0] * got[k]
            for j in range(1, 7):
                acc = acc + taps[j] * got[k - j]
            out.append(acc)
        return out

    def gates(l, first, last):
        a = short(1, l, first, last)
        b = short(2, l, first, last)
        for k in range(first, last):
            gate = (a[k - first] * b[k - first]).astype(BF16).astype(F32)
            gext[l, pl.ds(HALO + k, SUB, stride=span), :] = gate

    def queries(l, first, last):
        q = short(0, l, first, last)
        for k in range(first, last):
            qs[pl.ds(k * SUB, SUB), lanes(l)] = q[k - first]

    def own_gates(l, c):
        gates(l, 0, span)
        return c

    lax.fori_loop(0, tiles, own_gates, 0)

    def narrow(i, c):
        at = pl.multiple_of(i * 16, 16)
        for t in range(tiles):
            gsend[pl.ds(at, 16), pl.ds(t * 128, 128)] = gext[t, pl.ds(rows + at, 16), :].astype(BF16)
        return c

    lax.fori_loop(0, HALO // 16, narrow, 0)

    pl.semaphore_wait(barrier, n - 1)

    send_tail = pltpu.make_async_remote_copy(
        src_ref=x_ref.at[:, pl.ds(rows - 16, 16), :],
        dst_ref=tail,
        send_sem=halo_send.at[0],
        recv_sem=halo_recv.at[0],
        device_id={"ctx": nxt},
        device_id_type=MESH,
    )
    send_gate = pltpu.make_async_remote_copy(
        src_ref=gsend,
        dst_ref=ghalo,
        send_sem=halo_send.at[1],
        recv_sem=halo_recv.at[1],
        device_id={"ctx": nxt},
        device_id_type=MESH,
    )
    send_tail.start()
    send_gate.start()

    rate = rate_ref[...]
    angle = angle_ref[...]
    mag = jnp.exp(-rate)
    pr = mag * jnp.cos(angle)
    pi = mag * jnp.sin(angle)
    amp = jnp.sqrt(1.0 - jnp.exp(-2.0 * rate))
    rr = res_ref[0] * amp
    ri = res_ref[1] * amp
    put(pr_s, pr)
    put(pi_s, pi)
    put(a1_s, 2.0 * pr)
    put(a2_s, -(pr * pr + pi * pi))
    put(rr_s, rr)
    put(ri_s, ri)
    put(b1_s, -(rr * pr + ri * pi))

    def square(z):
        return z[0] * z[0] - z[1] * z[1], 2.0 * z[0] * z[1]

    z4 = square(square((pr, pi)))
    z16 = square(square(z4))
    z20 = (z16[0] * z4[0] - z16[1] * z4[1], z16[0] * z4[1] + z16[1] * z4[0])
    z40 = square(z20)
    z80 = square(z40)
    z160 = square(z80)
    for (fr, fi), z in zip(
        ((p20r, p20i), (p40r, p40i), (p80r, p80i), (p160r, p160i)), (z20, z40, z80, z160)
    ):
        put(fr, z[0])
        put(fi, z[1])

    sub = lax.broadcasted_iota(jnp.int32, (SUB, 128), 0)
    bits = [lax.rem(sub, 2) == 1, lax.rem(sub // 2, 2) == 1, sub >= 4]
    past = [sub >= 1, sub >= 2, sub >= 4]

    def powers(m, c):
        def at(l, cc):
            zr = jnp.where(bits[0], row(p20r, m, l), 1.0)
            zi = jnp.where(bits[0], row(p20i, m, l), 0.0)
            for bit, (fr, fi) in zip(bits[1:], ((p40r, p40i), (p80r, p80i))):
                ar = jnp.where(bit, row(fr, m, l), 1.0)
                ai = jnp.where(bit, row(fi, m, l), 0.0)
                zr, zi = zr * ar - zi * ai, zr * ai + zi * ar
            to = pl.ds(pl.multiple_of(m * SUB, SUB), SUB)
            qr[to, lanes(l)] = zr
            qi[to, lanes(l)] = zi
            return cc

        return lax.fori_loop(0, tiles, at, c)

    lax.fori_loop(0, modes, powers, 0)

    send_tail.wait_recv()
    for s in range(3):
        rim = jnp.where(me > 0, tail[s].astype(F32)[8:], 0.0)
        for t in range(tiles):
            xf[s * tiles + t, pl.ds(0, XH), :] = rim[:, t * 128 : (t + 1) * 128]

    def rim_rows(l, c):
        gates(l, 0, 6)
        queries(l, 0, span)
        return c

    lax.fori_loop(0, tiles, rim_rows, 0)

    send_gate.wait_recv()

    def rim_gates(i, c):
        at = pl.ds(pl.multiple_of(i * 16, 16), 16)
        rim = jnp.where(me > 0, ghalo[at, :].astype(F32), 0.0)
        for t in range(tiles):
            gext[t, at, :] = rim[:, t * 128 : (t + 1) * 128]
        return c

    lax.fori_loop(0, HALO // 16, rim_gates, 0)

    def first_send(q, dest):
        return pltpu.make_async_remote_copy(
            src_ref=ebuf.at[q],
            dst_ref=rbuf.at[me],
            send_sem=s1,
            recv_sem=r1,
            device_id={"ctx": dest},
            device_id_type=MESH,
        )

    def tile(l, c):
        def taps8(jb, acc):
            base = HALO - jb * 8
            taps = [row(mt_s, jb * 8 + jj, l) for jj in range(8)]
            got = {
                d: gext[l, pl.ds(base + d, SUB, stride=span), :]
                for d in range(-7, span)
            }
            out = []
            for k in range(span):
                v = acc[k]
                for jj in range(8):
                    v = v + taps[jj] * got[k - jj]
                out.append(v)
            return tuple(out)

        zero = jnp.zeros((SUB, 128), F32)
        acc = lax.fori_loop(0, HALO // 8, taps8, (zero,) * span)
        for k in range(span):
            med[pl.ds(k * SUB, SUB), lanes(l)] = acc[k]

        def ends(g, cc):
            ms = [g * GROUP + i for i in range(GROUP)]
            a1 = [row(a1_s, m, l) for m in ms]
            a2 = [row(a2_s, m, l) for m in ms]
            w1 = [zero] * GROUP
            w2 = [zero] * GROUP
            for k in range(span):
                x = med[pl.ds(k * SUB, SUB), lanes(l)]
                w = [x + a1[i] * w1[i] + a2[i] * w2[i] for i in range(GROUP)]
                w2 = w1
                w1 = w
            q = l * groups + g
            for i, m in enumerate(ms):
                er = w1[i] - row(pr_s, m, l) * w2[i]
                ei = row(pi_s, m, l) * w2[i]
                for d, keep, (fr, fi) in zip(
                    (1, 2, 4), past, ((p20r, p20i), (p40r, p40i), (p80r, p80i))
                ):
                    br = jnp.where(keep, pltpu.roll(er, d, 0), 0.0)
                    bi = jnp.where(keep, pltpu.roll(ei, d, 0), 0.0)
                    ar = row(fr, m, l)
                    ai = row(fi, m, l)
                    er, ei = er + ar * br - ai * bi, ei + ar * bi + ai * br
                to = pl.ds(pl.multiple_of(m * SUB, SUB), SUB)
                xr[to, lanes(l)] = jnp.where(past[0], pltpu.roll(er, 1, 0), 0.0)
                xi[to, lanes(l)] = jnp.where(past[0], pltpu.roll(ei, 1, 0), 0.0)
                ebuf[q, pl.ds(i, 1), :] = er[SUB - 1 :, :]
                ebuf[q, pl.ds(GROUP + i, 1), :] = ei[SUB - 1 :, :]
            dest = q * stride

            @pl.when(dest != me)
            def _():
                first_send(q, dest).start()

            @pl.when(dest == me)
            def _():
                rbuf[me] = ebuf[q]

            return cc

        return lax.fori_loop(0, groups, ends, c)

    lax.fori_loop(0, tiles, tile, 0)

    def local(l, c):
        def part(g, acc):
            out = list(acc)
            ms = [g * GROUP + i for i in range(GROUP)]
            a1 = [row(a1_s, m, l) for m in ms]
            a2 = [row(a2_s, m, l) for m in ms]
            b0 = [row(rr_s, m, l) for m in ms]
            b1 = [row(b1_s, m, l) for m in ms]
            zero = jnp.zeros((SUB, 128), F32)
            w1 = [zero] * GROUP
            w2 = [zero] * GROUP
            for k in range(span):
                x = med[pl.ds(k * SUB, SUB), lanes(l)]
                w = [x + a1[i] * w1[i] + a2[i] * w2[i] for i in range(GROUP)]
                for i in range(GROUP):
                    out[k] = out[k] + (b0[i] * w[i] + b1[i] * w1[i])
                w2 = w1
                w1 = w
            return tuple(out)

        skip = fixed_row(skip_ref, 0, l)
        acc = tuple(skip * med[pl.ds(k * SUB, SUB), lanes(l)] for k in range(span))
        acc = lax.fori_loop(0, groups, part, acc)
        for k in range(span):
            loc[pl.ds(k * SUB, SUB), lanes(l)] = acc[k]
        return c

    lax.fori_loop(0, tiles, local, 0)

    mine = me // stride
    scans = lax.rem(me, stride) == 0

    def reply(i):
        return pltpu.make_async_remote_copy(
            src_ref=obuf.at[i],
            dst_ref=sbuf.at[mine],
            send_sem=s2,
            recv_sem=r2,
            device_id={"ctx": i},
            device_id_type=MESH,
        )

    def await_tiles(ref, count, sem):
        part = ref.at[pl.ds(0, count)]
        pltpu.make_async_copy(part, part, sem).wait()

    @pl.when(scans)
    def _():
        await_tiles(rbuf, n - 1, r1)
        l = mine // groups
        g = lax.rem(mine, groups)
        dr = jnp.zeros((SUB, 128), F32)
        di = jnp.zeros((SUB, 128), F32)
        for i in range(GROUP):
            here = lax.rem(sub, GROUP) == i
            dr = jnp.where(here, row(p160r, g * GROUP + i, l), dr)
            di = jnp.where(here, row(p160i, g * GROUP + i, l), di)
        di = jnp.where(sub < GROUP, -di, di)

        def block(i, st):
            obuf[i] = st
            return dr * st + di * pltpu.roll(st, GROUP, 0) + rbuf[i]

        lax.fori_loop(0, n, block, jnp.zeros((SUB, 128), F32), unroll=8)

        def answer(r, c):
            reply(lax.rem(me + r, n)).start()
            return c

        lax.fori_loop(1, n, answer, 0)
        sbuf[mine] = obuf[me]
        await_tiles(sbuf, total - 1, r2)

    @pl.when(jnp.logical_not(scans))
    def _():
        await_tiles(sbuf, total, r2)

    def finish(l, c):
        def part(g, acc):
            out = list(acc)
            q = l * groups + g
            for i in range(GROUP):
                m = g * GROUP + i
                inr = jnp.broadcast_to(sbuf[q, pl.ds(i, 1), :], (SUB, 128))
                ini = jnp.broadcast_to(sbuf[q, pl.ds(GROUP + i, 1), :], (SUB, 128))
                at = pl.ds(pl.multiple_of(m * SUB, SUB), SUB)
                zr = qr[at, lanes(l)]
                zi = qi[at, lanes(l)]
                sr = xr[at, lanes(l)] + zr * inr - zi * ini
                si = xi[at, lanes(l)] + zr * ini + zi * inr
                rr = row(rr_s, m, l)
                ri = row(ri_s, m, l)
                ar = rr * sr - ri * si
                ai = rr * si + ri * sr
                u2 = ar
                u1 = ar * row(pr_s, m, l) - ai * row(pi_s, m, l)
                a1 = row(a1_s, m, l)
                a2 = row(a2_s, m, l)
                for k in range(span):
                    out[k] = out[k] + u1
                    u1, u2 = a1 * u1 + a2 * u2, u1
            return tuple(out)

        acc = tuple(loc[pl.ds(k * SUB, SUB), lanes(l)] for k in range(span))
        acc = lax.fori_loop(0, groups, part, acc)
        for k in range(span):
            hid = qs[pl.ds(k * SUB, SUB), lanes(l)] * acc[k]
            hid32[l, pl.ds(k, SUB, stride=span), :] = hid
        return c

    lax.fori_loop(0, tiles, finish, 0)

    def pack(i, c):
        at = pl.ds(pl.multiple_of(i * 16, 16), 16)
        for t in range(tiles):
            hid_ref[at, pl.ds(t * 128, 128)] = hid32[t, at, :].astype(BF16)
        return c

    lax.fori_loop(0, rows // 16, pack, 0)

    send_tail.wait_send()
    send_gate.wait_send()

    @pl.when(scans)
    def _():
        await_tiles(ebuf, total - 1, s1)
        await_tiles(obuf, n - 1, s2)

    @pl.when(jnp.logical_not(scans))
    def _():
        await_tiles(ebuf, total, s1)


def project_kernel(n, h_ref, w_ref, out_ref, sent, got, send_sem, recv_sem):
    rows, width = out_ref.shape
    me = lax.axis_index("tp")
    barrier = pltpu.get_barrier_semaphore()
    for r in range(1, n):
        pl.semaphore_signal(
            barrier, inc=1, device_id={"tp": lax.rem(me + r, n)}, device_id_type=MESH
        )

    def chunk(owner):
        cols = pl.ds(pl.multiple_of(owner * width, 128), width)
        return jnp.dot(h_ref[...], w_ref[:, cols], preferred_element_type=F32)

    copies = []
    for r in (2, 1, 3)[: n - 1] if n == 4 else range(1, n):
        to = lax.rem(me + r, n)
        sent[r - 1] = chunk(to).astype(BF16)
        if not copies:
            pl.semaphore_wait(barrier, n - 1)
        copy = pltpu.make_async_remote_copy(
            src_ref=sent.at[r - 1],
            dst_ref=got.at[r - 1],
            send_sem=send_sem.at[r - 1],
            recv_sem=recv_sem.at[r - 1],
            device_id={"tp": to},
            device_id_type=MESH,
        )
        copy.start()
        copies.append(copy)
    acc = chunk(me)
    for copy in copies:
        copy.wait_recv()
    for r in range(n - 1):
        acc = acc + got[r].astype(F32)
    out_ref[...] = acc.astype(BF16)
    for copy in copies:
        copy.wait_send()


def vmem(shape, dtype=F32):
    return pltpu.VMEM(shape, dtype)


def body(n_ctx, n_tp, streams, short_taps, mix_taps, pole_rate, pole_angle, residue, skip, out_weight):
    rows, three, width = streams.shape
    modes = pole_rate.shape[0]
    x = streams.transpose(1, 0, 2)
    staps = jnp.pad(short_taps.transpose(1, 0, 2), ((0, 0), (0, 1), (0, 0))).reshape(24, width)
    tiles = width // 128
    total = (modes // GROUP) * tiles
    coef = [vmem((tiles, modes, 128))] * 15
    vm = pl.BlockSpec(memory_space=pltpu.VMEM)
    weight = lax.all_gather(out_weight, "ctx", axis=1, tiled=True)
    hidden = pl.pallas_call(
        functools.partial(mixer_kernel, n_ctx),
        out_shape=jax.ShapeDtypeStruct((rows, width), BF16),
        in_specs=[vm] * 7,
        out_specs=vm,
        scratch_shapes=[
            vmem((3 * tiles, XH + rows, 128)),
            vmem((tiles, HALO + rows, 128)),
            vmem((HALO, width), BF16),
            vmem((HALO, width), BF16),
            vmem((3, 16, width), BF16),
            vmem((rows, width)),
            vmem((rows, width)),
            vmem((rows, width)),
            vmem((tiles, rows, 128)),
            vmem((modes * SUB, width)),
            vmem((modes * SUB, width)),
            vmem((modes * SUB, width)),
            vmem((modes * SUB, width)),
            *coef,
            vmem((tiles, HALO, 128)),
            vmem((total, 8, 128)),
            vmem((n_ctx, 8, 128)),
            vmem((n_ctx, 8, 128)),
            vmem((total, 8, 128)),
            pltpu.SemaphoreType.DMA((2,)),
            pltpu.SemaphoreType.DMA((2,)),
            pltpu.SemaphoreType.DMA,
            pltpu.SemaphoreType.DMA,
            pltpu.SemaphoreType.DMA,
            pltpu.SemaphoreType.DMA,
        ],
        compiler_params=pltpu.CompilerParams(collective_id=0, has_side_effects=True),
        name="mixer",
    )(x, staps, mix_taps, pole_rate, pole_angle, residue, skip[None])
    cols = weight.shape[1] // n_tp
    return pl.pallas_call(
        functools.partial(project_kernel, n_tp),
        out_shape=jax.ShapeDtypeStruct((rows, cols), BF16),
        in_specs=[vm] * 2,
        out_specs=vm,
        scratch_shapes=[
            vmem((n_tp - 1, rows, cols), BF16),
            vmem((n_tp - 1, rows, cols), BF16),
            pltpu.SemaphoreType.DMA((n_tp - 1,)),
            pltpu.SemaphoreType.DMA((n_tp - 1,)),
        ],
        compiler_params=pltpu.CompilerParams(collective_id=1, has_side_effects=True),
        name="project",
    )(hidden, weight)


def solution(mesh):
    return jax.shard_map(
        functools.partial(body, mesh.shape["ctx"], mesh.shape["tp"]),
        mesh=mesh,
        in_specs=(
            P("ctx", None, "tp"),
            P(None, None, "tp"),
            P(None, "tp"),
            P(None, "tp"),
            P(None, "tp"),
            P(None, None, "tp"),
            P("tp"),
            P("tp", "ctx"),
        ),
        out_specs=P("ctx", "tp"),
        check_vma=False,
    )
```

```python
import functools

import jax
import jax.numpy as jnp
from jax import lax
from jax.experimental import pallas as pl
from jax.experimental.pallas import tpu as pltpu
from jax.sharding import PartitionSpec as P

MESH = pl.DeviceIdType.MESH
SUB = 8
HALO = 128
XH = 8
GROUP = 4
F32 = jnp.float32
BF16 = jnp.bfloat16


def block_kernel(
    n,
    n_tp,
    x_ref,
    staps_ref,
    mtaps_ref,
    rate_ref,
    angle_ref,
    res_ref,
    skip_ref,
    w_ref,
    out_ref,
    xf,
    gext,
    gsend,
    ghalo,
    tail,
    qs,
    med,
    loc,
    hid32,
    xr,
    xi,
    qr,
    qi,
    pr_s,
    pi_s,
    a1_s,
    a2_s,
    rr_s,
    ri_s,
    b1_s,
    p20r,
    p20i,
    p40r,
    p40i,
    p80r,
    p80i,
    p160r,
    p160i,
    mt_s,
    ebuf,
    rbuf,
    obuf,
    sbuf,
    halo_send,
    halo_recv,
    s1,
    r1,
    s2,
    r2,
    wt,
    h2,
    own_sem,
    a1s,
    a1r,
    ps,
    pr_,
    ms,
    mr,
    h_send,
    h_recv,
    part,
    snd,
    rcv,
    rcvp,
    fin,
    y_send,
    y_recv,
    c_send,
    c_recv,
):
    _, rows, width = x_ref.shape
    n_x = n_tp
    n_z = n // (2 * n_x)
    wide = w_ref.shape[0]
    tp = lax.axis_index("tp")
    span = rows // SUB
    modes = rate_ref.shape[0]
    groups = modes // GROUP
    tiles = width // 128
    total = groups * tiles
    stride = n // total
    me = lax.axis_index("ctx")
    nxt = lax.rem(me + 1, n)
    core = lax.rem(me, 2)
    z = lax.rem(me // 2, n_z)
    x = me // (2 * n_z)
    other = me + 1 - 2 * core

    def at_x(dx):
        return lax.rem(x + dx + n_x, n_x)

    def at_z(dz):
        return lax.rem(z + dz + n_z, n_z)

    def device(xx, zz):
        return {"ctx": (xx * n_z + zz) * 2 + core}

    order = [0]
    for d in range(1, n_z // 2 + 1):
        order += [d] if 2 * d == n_z else [d, -d]

    own_block = pltpu.make_async_copy(w_ref, wt.at[x * n_z + z], own_sem)
    own_block.start()

    def along_z(dz):
        return pltpu.make_async_remote_copy(
            src_ref=w_ref,
            dst_ref=wt.at[x * n_z + z],
            send_sem=a1s.at[dz % n_z],
            recv_sem=a1r.at[(-dz) % n_z],
            device_id=device(x, at_z(dz)),
            device_id_type=MESH,
        )

    def from_z(dz):
        block = wt.at[x * n_z + at_z(dz)]
        return pltpu.make_async_copy(block, block, a1r.at[dz % n_z])

    def along_x(step, hop, p):
        send, recv = (ps, pr_) if step > 0 else (ms, mr)
        block = wt.at[at_x(-step * hop) * n_z + at_z(order[p])]
        return pltpu.make_async_remote_copy(
            src_ref=block,
            dst_ref=block,
            send_sem=send.at[hop * n_z + p],
            recv_sem=recv.at[hop * n_z + p],
            device_id=device(at_x(step), z),
            device_id_type=MESH,
        )

    def from_x(step, hop, p):
        recv = pr_ if step > 0 else mr
        block = wt.at[at_x(-step * (hop + 1)) * n_z + at_z(order[p])]
        return pltpu.make_async_copy(block, block, recv.at[hop * n_z + p])

    steps = (1, -1) if n_x > 2 else (1,)
    passed = {1: [], -1: []}
    if n_x == 4:
        passed = {1: [p for p in range(n_z) if p % 2 == 0], -1: [p for p in range(n_z) if p % 2 == 1]}
    started = []

    def give(*ps_):
        for p in ps_:
            if p < n_z:
                if p:
                    from_z(order[p]).wait()
                for step in steps:
                    along_x(step, 0, p).start()
                    started.append((step, 0, p))

    def hand_on(step, *ps_):
        for p in ps_:
            if p in passed[step]:
                from_x(step, 0, p).wait()
                along_x(step, 1, p).start()
                started.append((step, 1, p))

    def lanes(l):
        return pl.ds(pl.multiple_of(l * 128, 128), 128)

    def fixed_row(ref, r, l):
        return jnp.broadcast_to(ref[pl.ds(r, 1), lanes(l)], (SUB, 128))

    def row(ref, r, l):
        return ref[l, pl.ds(r, SUB, stride=0), :]

    def put(ref, value):
        for t in range(tiles):
            ref[t] = value[:, t * 128 : (t + 1) * 128]

    barrier = pltpu.get_barrier_semaphore()

    def greet(r, c):
        pl.semaphore_signal(
            barrier, inc=1, device_id={"ctx": lax.rem(me + r, n)}, device_id_type=MESH
        )
        return c

    lax.fori_loop(1, n, greet, 0)
    for r in range(1, n_tp):
        for who in (me, other):
            pl.semaphore_signal(
                barrier,
                inc=1,
                device_id={"ctx": who, "tp": lax.rem(tp + r, n_tp)},
                device_id_type=MESH,
            )

    for t in range(tiles):
        mt_s[t] = mtaps_ref[:, pl.ds(t * 128, 128)]

    for s in range(3):
        for t in range(tiles):
            xf[s * tiles + t, pl.ds(0, XH), :] = jnp.zeros((XH, 128), F32)

        def widen(i, c, s=s):
            at = pl.multiple_of(i * 16, 16)
            to = pl.multiple_of(XH + i * 16, 8)
            block = x_ref[s, pl.ds(at, 16), :].astype(F32)
            for t in range(tiles):
                xf[s * tiles + t, pl.ds(to, 16), :] = block[:, t * 128 : (t + 1) * 128]
            return c

        lax.fori_loop(0, rows // 16, widen, 0)

    def short(s, l, first, last):
        taps = [jnp.broadcast_to(staps_ref[s, pl.ds(j, 1), lanes(l)], (SUB, 128)) for j in range(7)]
        got = {}
        for d in range(first - 6, last):
            got[d] = xf[s * tiles + l, pl.ds(XH + d, SUB, stride=span), :]
        out = []
        for k in range(first, last):
            acc = taps[0] * got[k]
            for j in range(1, 7):
                acc = acc + taps[j] * got[k - j]
            out.append(acc)
        return out

    def gates(l, first, last):
        a = short(1, l, first, last)
        b = short(2, l, first, last)
        for k in range(first, last):
            gate = (a[k - first] * b[k - first]).astype(BF16).astype(F32)
            gext[l, pl.ds(HALO + k, SUB, stride=span), :] = gate

    def queries(l, first, last):
        q = short(0, l, first, last)
        for k in range(first, last):
            qs[pl.ds(k * SUB, SUB), lanes(l)] = q[k - first]

    def own_gates(l, c):
        gates(l, 0, span)
        return c

    lax.fori_loop(0, tiles, own_gates, 0)

    def narrow(i, c):
        at = pl.multiple_of(i * 16, 16)
        for t in range(tiles):
            gsend[pl.ds(at, 16), pl.ds(t * 128, 128)] = gext[t, pl.ds(rows + at, 16), :].astype(BF16)
        return c

    lax.fori_loop(0, HALO // 16, narrow, 0)

    pl.semaphore_wait(barrier, n - 1 + 2 * (n_tp - 1))

    send_tail = pltpu.make_async_remote_copy(
        src_ref=x_ref.at[:, pl.ds(rows - 16, 16), :],
        dst_ref=tail,
        send_sem=halo_send.at[0],
        recv_sem=halo_recv.at[0],
        device_id={"ctx": nxt},
        device_id_type=MESH,
    )
    send_gate = pltpu.make_async_remote_copy(
        src_ref=gsend,
        dst_ref=ghalo,
        send_sem=halo_send.at[1],
        recv_sem=halo_recv.at[1],
        device_id={"ctx": nxt},
        device_id_type=MESH,
    )
    send_tail.start()
    send_gate.start()

    rate = rate_ref[...]
    angle = angle_ref[...]
    mag = jnp.exp(-rate)
    pr = mag * jnp.cos(angle)
    pi = mag * jnp.sin(angle)
    amp = jnp.sqrt(1.0 - jnp.exp(-2.0 * rate))
    rr = res_ref[0] * amp
    ri = res_ref[1] * amp
    put(pr_s, pr)
    put(pi_s, pi)
    put(a1_s, 2.0 * pr)
    put(a2_s, -(pr * pr + pi * pi))
    put(rr_s, rr)
    put(ri_s, ri)
    put(b1_s, -(rr * pr + ri * pi))

    def square(z):
        return z[0] * z[0] - z[1] * z[1], 2.0 * z[0] * z[1]

    z4 = square(square((pr, pi)))
    z16 = square(square(z4))
    z20 = (z16[0] * z4[0] - z16[1] * z4[1], z16[0] * z4[1] + z16[1] * z4[0])
    z40 = square(z20)
    z80 = square(z40)
    z160 = square(z80)
    for (fr, fi), power in zip(
        ((p20r, p20i), (p40r, p40i), (p80r, p80i), (p160r, p160i)), (z20, z40, z80, z160)
    ):
        put(fr, power[0])
        put(fi, power[1])

    sub = lax.broadcasted_iota(jnp.int32, (SUB, 128), 0)
    bits = [lax.rem(sub, 2) == 1, lax.rem(sub // 2, 2) == 1, sub >= 4]
    past = [sub >= 1, sub >= 2, sub >= 4]

    def powers(m, c):
        def at(l, cc):
            zr = jnp.where(bits[0], row(p20r, m, l), 1.0)
            zi = jnp.where(bits[0], row(p20i, m, l), 0.0)
            for bit, (fr, fi) in zip(bits[1:], ((p40r, p40i), (p80r, p80i))):
                ar = jnp.where(bit, row(fr, m, l), 1.0)
                ai = jnp.where(bit, row(fi, m, l), 0.0)
                zr, zi = zr * ar - zi * ai, zr * ai + zi * ar
            to = pl.ds(pl.multiple_of(m * SUB, SUB), SUB)
            qr[to, lanes(l)] = zr
            qi[to, lanes(l)] = zi
            return cc

        return lax.fori_loop(0, tiles, at, c)

    lax.fori_loop(0, modes, powers, 0)

    send_tail.wait_recv()
    for s in range(3):
        rim = jnp.where(me > 0, tail[s].astype(F32)[8:], 0.0)
        for t in range(tiles):
            xf[s * tiles + t, pl.ds(0, XH), :] = rim[:, t * 128 : (t + 1) * 128]

    def rim_rows(l, c):
        gates(l, 0, 6)
        queries(l, 0, span)
        return c

    lax.fori_loop(0, tiles, rim_rows, 0)

    send_gate.wait_recv()

    def rim_gates(i, c):
        at = pl.ds(pl.multiple_of(i * 16, 16), 16)
        rim = jnp.where(me > 0, ghalo[at, :].astype(F32), 0.0)
        for t in range(tiles):
            gext[t, at, :] = rim[:, t * 128 : (t + 1) * 128]
        return c

    lax.fori_loop(0, HALO // 16, rim_gates, 0)

    own_block.wait()
    give(0)
    for dz in order[1:]:
        along_z(dz).start()

    def first_send(q, dest):
        return pltpu.make_async_remote_copy(
            src_ref=ebuf.at[q],
            dst_ref=rbuf.at[me],
            send_sem=s1,
            recv_sem=r1,
            device_id={"ctx": dest},
            device_id_type=MESH,
        )

    def tile(l, c):
        def taps8(jb, acc):
            base = HALO - jb * 8
            taps = [row(mt_s, jb * 8 + jj, l) for jj in range(8)]
            got = {
                d: gext[l, pl.ds(base + d, SUB, stride=span), :]
                for d in range(-7, span)
            }
            out = []
            for k in range(span):
                v = acc[k]
                for jj in range(8):
                    v = v + taps[jj] * got[k - jj]
                out.append(v)
            return tuple(out)

        zero = jnp.zeros((SUB, 128), F32)
        acc = lax.fori_loop(0, HALO // 8, taps8, (zero,) * span)
        for k in range(span):
            med[pl.ds(k * SUB, SUB), lanes(l)] = acc[k]

        def ends(g, cc):
            ms = [g * GROUP + i for i in range(GROUP)]
            a1 = [row(a1_s, m, l) for m in ms]
            a2 = [row(a2_s, m, l) for m in ms]
            w1 = [zero] * GROUP
            w2 = [zero] * GROUP
            for k in range(span):
                x = med[pl.ds(k * SUB, SUB), lanes(l)]
                w = [x + a1[i] * w1[i] + a2[i] * w2[i] for i in range(GROUP)]
                w2 = w1
                w1 = w
            q = l * groups + g
            for i, m in enumerate(ms):
                er = w1[i] - row(pr_s, m, l) * w2[i]
                ei = row(pi_s, m, l) * w2[i]
                for d, keep, (fr, fi) in zip(
                    (1, 2, 4), past, ((p20r, p20i), (p40r, p40i), (p80r, p80i))
                ):
                    br = jnp.where(keep, pltpu.roll(er, d, 0), 0.0)
                    bi = jnp.where(keep, pltpu.roll(ei, d, 0), 0.0)
                    ar = row(fr, m, l)
                    ai = row(fi, m, l)
                    er, ei = er + ar * br - ai * bi, ei + ar * bi + ai * br
                to = pl.ds(pl.multiple_of(m * SUB, SUB), SUB)
                xr[to, lanes(l)] = jnp.where(past[0], pltpu.roll(er, 1, 0), 0.0)
                xi[to, lanes(l)] = jnp.where(past[0], pltpu.roll(ei, 1, 0), 0.0)
                ebuf[q, pl.ds(i, 1), :] = er[SUB - 1 :, :]
                ebuf[q, pl.ds(GROUP + i, 1), :] = ei[SUB - 1 :, :]
            dest = q * stride

            @pl.when(dest != me)
            def _():
                first_send(q, dest).start()

            @pl.when(dest == me)
            def _():
                rbuf[me] = ebuf[q]

            return cc

        return lax.fori_loop(0, groups, ends, c)

    lax.fori_loop(0, tiles, tile, 0)

    give(1, 2)
    hand_on(1, 0)

    def local(l, c):
        def part(g, acc):
            out = list(acc)
            ms = [g * GROUP + i for i in range(GROUP)]
            a1 = [row(a1_s, m, l) for m in ms]
            a2 = [row(a2_s, m, l) for m in ms]
            b0 = [row(rr_s, m, l) for m in ms]
            b1 = [row(b1_s, m, l) for m in ms]
            zero = jnp.zeros((SUB, 128), F32)
            w1 = [zero] * GROUP
            w2 = [zero] * GROUP
            for k in range(span):
                x = med[pl.ds(k * SUB, SUB), lanes(l)]
                w = [x + a1[i] * w1[i] + a2[i] * w2[i] for i in range(GROUP)]
                for i in range(GROUP):
                    out[k] = out[k] + (b0[i] * w[i] + b1[i] * w1[i])
                w2 = w1
                w1 = w
            return tuple(out)

        skip = fixed_row(skip_ref, 0, l)
        acc = tuple(skip * med[pl.ds(k * SUB, SUB), lanes(l)] for k in range(span))
        acc = lax.fori_loop(0, groups, part, acc)
        for k in range(span):
            loc[pl.ds(k * SUB, SUB), lanes(l)] = acc[k]
        return c

    lax.fori_loop(0, tiles, local, 0)

    give(3, 4)
    hand_on(1, 2)
    hand_on(-1, 1)

    mine = me // stride
    scans = lax.rem(me, stride) == 0

    def reply(i):
        return pltpu.make_async_remote_copy(
            src_ref=obuf.at[i],
            dst_ref=sbuf.at[mine],
            send_sem=s2,
            recv_sem=r2,
            device_id={"ctx": i},
            device_id_type=MESH,
        )

    def await_tiles(ref, count, sem):
        part = ref.at[pl.ds(0, count)]
        pltpu.make_async_copy(part, part, sem).wait()

    @pl.when(scans)
    def _():
        await_tiles(rbuf, n - 1, r1)
        l = mine // groups
        g = lax.rem(mine, groups)
        dr = jnp.zeros((SUB, 128), F32)
        di = jnp.zeros((SUB, 128), F32)
        for i in range(GROUP):
            here = lax.rem(sub, GROUP) == i
            dr = jnp.where(here, row(p160r, g * GROUP + i, l), dr)
            di = jnp.where(here, row(p160i, g * GROUP + i, l), di)
        di = jnp.where(sub < GROUP, -di, di)

        def block(i, st):
            obuf[i] = st
            return dr * st + di * pltpu.roll(st, GROUP, 0) + rbuf[i]

        lax.fori_loop(0, n, block, jnp.zeros((SUB, 128), F32), unroll=8)

        def answer(r, c):
            reply(lax.rem(me + r, n)).start()
            return c

        lax.fori_loop(1, n, answer, 0)
        sbuf[mine] = obuf[me]

    give(5, 6)
    hand_on(1, 4)
    hand_on(-1, 3)

    @pl.when(scans)
    def _():
        await_tiles(sbuf, total - 1, r2)

    @pl.when(jnp.logical_not(scans))
    def _():
        await_tiles(sbuf, total, r2)

    def finish(l, c):
        def part(g, acc):
            out = list(acc)
            q = l * groups + g
            for i in range(GROUP):
                m = g * GROUP + i
                inr = jnp.broadcast_to(sbuf[q, pl.ds(i, 1), :], (SUB, 128))
                ini = jnp.broadcast_to(sbuf[q, pl.ds(GROUP + i, 1), :], (SUB, 128))
                at = pl.ds(pl.multiple_of(m * SUB, SUB), SUB)
                zr = qr[at, lanes(l)]
                zi = qi[at, lanes(l)]
                sr = xr[at, lanes(l)] + zr * inr - zi * ini
                si = xi[at, lanes(l)] + zr * ini + zi * inr
                rr = row(rr_s, m, l)
                ri = row(ri_s, m, l)
                ar = rr * sr - ri * si
                ai = rr * si + ri * sr
                u2 = ar
                u1 = ar * row(pr_s, m, l) - ai * row(pi_s, m, l)
                a1 = row(a1_s, m, l)
                a2 = row(a2_s, m, l)
                for k in range(span):
                    out[k] = out[k] + u1
                    u1, u2 = a1 * u1 + a2 * u2, u1
            return tuple(out)

        acc = tuple(loc[pl.ds(k * SUB, SUB), lanes(l)] for k in range(span))
        acc = lax.fori_loop(0, groups, part, acc)
        for k in range(span):
            hid = qs[pl.ds(k * SUB, SUB), lanes(l)] * acc[k]
            hid32[l, pl.ds(k, SUB, stride=span), :] = hid
        h2[core, :, lanes(l)] = hid32[l].astype(BF16)
        send_hidden(l).start()
        return c

    def send_hidden(l):
        return pltpu.make_async_remote_copy(
            src_ref=h2.at[core, :, lanes(l)],
            dst_ref=h2.at[core, :, lanes(l)],
            send_sem=h_send,
            recv_sem=h_recv,
            device_id={"ctx": other},
            device_id_type=MESH,
        )

    lax.fori_loop(0, tiles, finish, 0)

    give(*range(7, n_z))
    hand_on(-1, 5)
    hand_on(1, 6)
    hand_on(-1, 7)
    pltpu.make_async_copy(h2.at[1 - core], h2.at[1 - core], h_recv).wait()

    half = n_z * wide

    def to_y(k, to, r):
        return [
            pltpu.make_async_remote_copy(
                src_ref=snd.at[k, cc],
                dst_ref=rcv.at[r - 1, core],
                send_sem=y_send.at[k, cc],
                recv_sem=y_recv.at[r - 1, core],
                device_id={"ctx": me - core + cc, "tp": to},
                device_id_type=MESH,
            )
            for cc in range(2)
        ]

    to_core = pltpu.make_async_remote_copy(
        src_ref=part.at[1 - core],
        dst_ref=rcvp,
        send_sem=c_send,
        recv_sem=c_recv,
        device_id={"ctx": other},
        device_id_type=MESH,
    )
    turns = [0, 1, -1, 2][:n_x] if n_x == 4 else list(range(n_x))
    for k, dx in enumerate(turns):
        if dx == 1 and n_x == 4:
            for p in range(n_z):
                if p not in passed[-1]:
                    from_x(-1, 0, p).wait()
        elif dx == -1 or dx == 1:
            for p in range(n_z):
                if p not in passed[1]:
                    from_x(1, 0, p).wait()
        elif dx == 2:
            for step in steps:
                for p in passed[step]:
                    from_x(step, 1, p).wait()
        to = at_x(dx)
        r = lax.rem(to - tp + n_tp, n_tp)
        w = wt[pl.ds(to * n_z, n_z)].reshape(half, width)
        for cc in range(2):
            got = lax.dot_general(
                h2[cc], w, (((1,), (1,)), ((), ())), preferred_element_type=F32
            )

            @pl.when(r == 0)
            def _(got=got, cc=cc):
                part[cc] = got

            @pl.when(r != 0)
            def _(got=got, cc=cc, k=k):
                snd[k, cc] = got.astype(BF16)

        @pl.when(r == 0)
        def _():
            to_core.start()

        @pl.when(r != 0)
        def _(k=k, to=to, r=r):
            for copy in to_y(k, to, r):
                copy.start()

    def got_from(r, cc):
        block = rcv.at[r - 1, cc]
        pltpu.make_async_copy(block, block, y_recv.at[r - 1, cc]).wait()

    to_core.wait_recv()
    for r in range(1, n_tp):
        for cc in range(2):
            got_from(r, cc)

    def add(i, c):
        at = pl.ds(pl.multiple_of(i * 16, 16), 16)
        mine_sum = part[core, at, :]
        other_sum = rcvp[at, :]
        for r in range(1, n_tp):
            mine_sum = mine_sum + rcv[r - 1, core, at, :].astype(F32)
            other_sum = other_sum + rcv[r - 1, 1 - core, at, :].astype(F32)
        fin[core, at, :] = mine_sum
        fin[1 - core, at, :] = other_sum
        low = lax.broadcasted_iota(jnp.int32, (16, 128), 1) < wide
        for t in range(half // 128):
            a = fin[0, at, pl.ds(t * 128, 128)]
            b = fin[1, at, pl.ds(t * 128, 128)]
            out_ref[at, pl.ds(t * 256, 128)] = jnp.where(low, a, pltpu.roll(b, wide, 1)).astype(BF16)
            out_ref[at, pl.ds(t * 256 + 128, 128)] = jnp.where(low, pltpu.roll(a, wide, 1), b).astype(BF16)
        return c

    lax.fori_loop(0, rows // 16, add, 0)

    for dz in order[1:]:
        along_z(dz).wait_send()
    for what in started:
        along_x(*what).wait_send()
    pltpu.make_async_copy(h2.at[core], h2.at[core], h_send).wait()
    to_core.wait_send()
    for k, dx in enumerate(turns):
        to = at_x(dx)
        r = lax.rem(to - tp + n_tp, n_tp)

        @pl.when(r != 0)
        def _(k=k, to=to, r=r):
            for copy in to_y(k, to, r):
                copy.wait_send()

    send_tail.wait_send()
    send_gate.wait_send()

    @pl.when(scans)
    def _():
        await_tiles(ebuf, total - 1, s1)
        await_tiles(obuf, n - 1, s2)

    @pl.when(jnp.logical_not(scans))
    def _():
        await_tiles(ebuf, total, s1)


def vmem(shape, dtype=F32):
    return pltpu.VMEM(shape, dtype)


def body(n_ctx, n_tp, streams, short_taps, mix_taps, pole_rate, pole_angle, residue, skip, out_weight):
    rows, three, width = streams.shape
    modes = pole_rate.shape[0]
    tiles = width // 128
    total = (modes // GROUP) * tiles
    cols = out_weight.shape[1]
    half = n_ctx // (2 * n_tp) * cols
    coef = [vmem((tiles, modes, 128))] * 15
    vm = pl.BlockSpec(memory_space=pltpu.VMEM)
    hbm = pl.BlockSpec(memory_space=pl.ANY)
    return pl.pallas_call(
        functools.partial(block_kernel, n_ctx, n_tp),
        out_shape=jax.ShapeDtypeStruct((rows, 2 * half), BF16),
        in_specs=[vm] * 7 + [hbm],
        out_specs=vm,
        scratch_shapes=[
            vmem((3 * tiles, XH + rows, 128)),
            vmem((tiles, HALO + rows, 128)),
            vmem((HALO, width), BF16),
            vmem((HALO, width), BF16),
            vmem((3, 16, width), BF16),
            vmem((rows, width)),
            vmem((rows, width)),
            vmem((rows, width)),
            vmem((tiles, rows, 128)),
            vmem((modes * SUB, width)),
            vmem((modes * SUB, width)),
            vmem((modes * SUB, width)),
            vmem((modes * SUB, width)),
            *coef,
            vmem((tiles, HALO, 128)),
            vmem((total, 8, 128)),
            vmem((n_ctx, 8, 128)),
            vmem((n_ctx, 8, 128)),
            vmem((total, 8, 128)),
            pltpu.SemaphoreType.DMA((2,)),
            pltpu.SemaphoreType.DMA((2,)),
            pltpu.SemaphoreType.DMA,
            pltpu.SemaphoreType.DMA,
            pltpu.SemaphoreType.DMA,
            pltpu.SemaphoreType.DMA,
            vmem((n_ctx // 2, cols, width), BF16),
            vmem((2, rows, width), BF16),
            pltpu.SemaphoreType.DMA,
            *[pltpu.SemaphoreType.DMA((n_ctx // n_tp,))] * 6,
            pltpu.SemaphoreType.DMA,
            pltpu.SemaphoreType.DMA,
            vmem((2, rows, half)),
            vmem((n_tp, 2, rows, half), BF16),
            vmem((n_tp - 1, 2, rows, half), BF16),
            vmem((rows, half)),
            vmem((2, rows, half)),
            pltpu.SemaphoreType.DMA((n_tp, 2)),
            pltpu.SemaphoreType.DMA((n_tp - 1, 2)),
            pltpu.SemaphoreType.DMA,
            pltpu.SemaphoreType.DMA,
        ],
        compiler_params=pltpu.CompilerParams(collective_id=0, has_side_effects=True),
        name="hyena_block",
    )(
        streams.transpose(1, 0, 2),
        short_taps.transpose(1, 0, 2),
        mix_taps,
        pole_rate,
        pole_angle,
        residue,
        skip[None],
        out_weight.T,
    )


def solution(mesh):
    return jax.shard_map(
        functools.partial(body, mesh.shape["ctx"], mesh.shape["tp"]),
        mesh=mesh,
        in_specs=(
            P("ctx", None, "tp"),
            P(None, None, "tp"),
            P(None, "tp"),
            P(None, "tp"),
            P(None, "tp"),
            P(None, None, "tp"),
            P("tp"),
            P("tp", "ctx"),
        ),
        out_specs=P("ctx", "tp"),
        check_vma=False,
    )
```

```python
import functools

import jax
import jax.numpy as jnp
from jax import lax
from jax.experimental import pallas as pl
from jax.experimental.pallas import tpu as pltpu
from jax.sharding import PartitionSpec as P

MESH = pl.DeviceIdType.MESH
SUB = 8
HALO = 128
XH = 8
GROUP = 4
F32 = jnp.float32
BF16 = jnp.bfloat16


def block_kernel(
    n,
    n_tp,
    x_hbm,
    staps_hbm,
    mtaps_hbm,
    rate_hbm,
    angle_hbm,
    res_hbm,
    skip_hbm,
    w_ref,
    out_ref,
    x_ref,
    staps_ref,
    mtaps_ref,
    rate_ref,
    angle_ref,
    res_ref,
    skip_ref,
    in_sem,
    xf,
    gext,
    gsend,
    ghalo,
    tail,
    qs,
    med,
    loc,
    hid32,
    xr,
    xi,
    qr,
    qi,
    pr_s,
    pi_s,
    a1_s,
    a2_s,
    rr_s,
    ri_s,
    b1_s,
    p20r,
    p20i,
    p40r,
    p40i,
    p80r,
    p80i,
    p160r,
    p160i,
    mt_s,
    ebuf,
    rbuf,
    obuf,
    sbuf,
    tot,
    t_send,
    t_recv,
    halo_send,
    halo_recv,
    s1,
    r1,
    s2,
    r2,
    wt,
    h2,
    own_sem,
    w_send,
    w_recv,
    h_send,
    h_recv,
    part,
    snd,
    rel,
    rcv,
    rcvp,
    hold,
    y_send,
    y_recv,
    v_recv,
    c_send,
    c_recv,
):
    _, rows, width = x_ref.shape
    n_x = n_tp
    n_z = n // (2 * n_x)
    wide = w_ref.shape[0]
    tp = lax.axis_index("tp")
    span = rows // SUB
    modes = rate_ref.shape[0]
    groups = modes // GROUP
    tiles = width // 128
    total = groups * tiles
    line = n // n_tp
    each = total // line
    me = lax.axis_index("ctx")
    nxt = lax.rem(me + 1, n)
    core = lax.rem(me, 2)
    z = lax.rem(me // 2, n_z)
    x = me // (2 * n_z)
    other = me + 1 - 2 * core

    def at_x(dx):
        return lax.rem(x + dx + n_x, n_x)

    def at_z(dz):
        return lax.rem(z + dz + n_z, n_z)

    def device(xx, zz):
        return {"ctx": (xx * n_z + zz) * 2 + core}

    cut = 3 * w_ref.shape[0] // 4
    parts_ = (pl.ds(0, cut), pl.ds(cut, w_ref.shape[0] - cut))
    dxs = [0]
    for d in range(1, n_x // 2 + 1):
        dxs += [d] if 2 * d == n_x else [d, -d]
    order = [0]
    for d in range(1, n_z // 2 + 1):
        order += [d] if 2 * d == n_z else [d, -d]
    far_z, far_x = n_z // 2, n_x // 2
    own = x * n_z + z
    own_block = pltpu.make_async_copy(w_ref, wt.at[own], own_sem)

    def piece(half_, dx, dz):
        return wt.at[at_x(dx) * n_z + at_z(dz), parts_[half_], :]

    def slot(half_, dx, dz):
        return (half_ * n_x + dx % n_x) * n_z + dz % n_z

    waited = {slot(0, 0, 0), slot(1, 0, 0)}
    sends = []

    def need(half_, dx, dz):
        if slot(half_, dx, dz) not in waited:
            waited.add(slot(half_, dx, dz))
            block = piece(half_, dx, dz)
            pltpu.make_async_copy(block, block, w_recv.at[slot(half_, dx, dz)]).wait()

    def pass_on(half_, dx, dz, sx, sz, count):
        block = piece(half_, dx, dz)
        return pltpu.make_async_remote_copy(
            src_ref=block,
            dst_ref=block,
            send_sem=w_send.at[count],
            recv_sem=w_recv.at[slot(half_, dx - sx, dz - sz)],
            device_id=device(at_x(sx), at_z(sz)),
            device_id_type=MESH,
        )

    def push(half_, dx, dz, sx, sz):
        need(half_, dx, dz)
        what = (half_, dx, dz, sx, sz, len(sends))
        sends.append(what)
        pass_on(*what).start()

    def direct():
        for sx in dxs[1:]:
            push(1, 0, 0, sx, 0)
        for sx in dxs[1:]:
            push(0, 0, 0, sx, 0)

    def direct_z():
        for sz in order[1:5]:
            push(0, 0, 0, 0, sz)
        z_then(0, 0)

    def z_far():
        if n_z == 8:
            push(0, 0, -2, 0, 1)
            push(0, 0, 2, 0, -1)
            push(0, 0, -2, 0, 2)

    def x_then(*ps):
        for p in ps:
            if p < n_z:
                push(0, 0, order[p], 1, 0)
                if n_x > 2:
                    push(0, 0, order[p], -1, 0)

    def x_relay(*ps):
        for p in ps:
            if p < n_z and n_x > 2:
                step = 1 if p % 2 == 0 else -1
                push(0, -step, order[p], step, 0)

    def z_then(h, *js):
        for j in js:
            if j < n_x:
                last = h == far_z - 1
                if h < far_z and (not last or j < n_x // 2 or n_z % 2):
                    push(1, dxs[j], -h, 0, 1)
                if h < far_z and (not last or j >= n_x // 2):
                    push(1, dxs[j], h, 0, -1)

    plan = {turn: [] for turn in range(21)}
    plan[0] = [(direct,)]
    plan[3] = [(direct_z,)]
    plan[8] = [(z_then, 0, 1, 2, 3)]
    plan[9] = [(x_then, 1, 2)]
    plan[12] = [(x_then, 3, 4)]
    plan[13] = [(z_far,)]
    plan[15] = [(x_relay, 1, 2)]
    plan[16] = [(x_relay, 3, 4), (x_then, 5, 6, 7)]
    plan[20] = [(z_then, 1, 0, 1, 2, 3)]
    plan[17] = [(z_then, 2, 0, 1, 2, 3)]
    plan[18] = [(x_relay, 5, 6, 7)]
    plan[19] = [(z_then, 3, 0, 1, 2, 3)]

    def serve(turn):
        for what, *args in plan[turn]:
            what(*args)

    def serve_in(l, first, count, every=1):
        if l % every == 0 and l // every < count:
            serve(first + l // every)

    def lanes(l):
        return pl.ds(l * 128 if isinstance(l, int) else pl.multiple_of(l * 128, 128), 128)

    def fixed_row(ref, r, l):
        return jnp.broadcast_to(ref[pl.ds(r, 1), lanes(l)], (SUB, 128))

    def row(ref, r, l):
        return ref[l, pl.ds(r, SUB, stride=0), :]

    def put(ref, value):
        for t in range(tiles):
            ref[t] = value[:, t * 128 : (t + 1) * 128]

    barrier = pltpu.get_barrier_semaphore()
    hbm = (x_hbm, staps_hbm, mtaps_hbm, rate_hbm, angle_hbm, res_hbm, skip_hbm)
    here = (x_ref, staps_ref, mtaps_ref, rate_ref, angle_ref, res_ref, skip_ref)
    loads = [pltpu.make_async_copy(a, b, in_sem.at[i]) for i, (a, b) in enumerate(zip(hbm, here))]
    for load in loads:
        load.start()
    own_block.start()

    spot = lax.rem(me, line)

    def on_line(i):
        return {"ctx": x * line + i}

    def greet(where):
        pl.semaphore_signal(barrier, inc=1, device_id=where, device_id_type=MESH)

    for r in (1, n - 1):
        greet({"ctx": lax.rem(me + r, n)})
    for r in range(1, line):
        greet(on_line(lax.rem(spot + r, line)))
    for dx in range(1, n_x):
        greet(device(at_x(dx), z))
    for r in range(1, n_tp):
        for who in (me, other):
            pl.semaphore_signal(
                barrier,
                inc=1,
                device_id={"ctx": who, "tp": lax.rem(tp + r, n_tp)},
                device_id_type=MESH,
            )

    loads[0].wait()
    loads[1].wait()
    for s in range(3):
        for t in range(tiles):
            xf[s * tiles + t, pl.ds(0, XH), :] = jnp.zeros((XH, 128), F32)

        def widen(i, c, s=s):
            at = pl.multiple_of(i * 16, 16)
            to = pl.multiple_of(XH + i * 16, 8)
            block = x_ref[s, pl.ds(at, 16), :].astype(F32)
            for t in range(tiles):
                xf[s * tiles + t, pl.ds(to, 16), :] = block[:, t * 128 : (t + 1) * 128]
            return c

        lax.fori_loop(0, rows // 16, widen, 0)

    def short(s, l, first, last):
        taps = [jnp.broadcast_to(staps_ref[s, pl.ds(j, 1), lanes(l)], (SUB, 128)) for j in range(7)]
        got = {}
        for d in range(first - 6, last):
            got[d] = xf[s * tiles + l, pl.ds(XH + d, SUB, stride=span), :]
        out = []
        for k in range(first, last):
            acc = taps[0] * got[k]
            for j in range(1, 7):
                acc = acc + taps[j] * got[k - j]
            out.append(acc)
        return out

    def gates(l, first, last):
        a = short(1, l, first, last)
        b = short(2, l, first, last)
        for k in range(first, last):
            gate = (a[k - first] * b[k - first]).astype(BF16).astype(F32)
            gext[l, pl.ds(HALO + k, SUB, stride=span), :] = gate

    def queries(l, first, last):
        q = short(0, l, first, last)
        for k in range(first, last):
            qs[pl.ds(k * SUB, SUB), lanes(l)] = q[k - first]

    def own_gates(l, c):
        gates(l, 0, span)
        return c

    lax.fori_loop(0, tiles, own_gates, 0)

    def narrow(i, c):
        at = pl.multiple_of(i * 16, 16)
        for t in range(tiles):
            gsend[pl.ds(at, 16), pl.ds(t * 128, 128)] = gext[t, pl.ds(rows + at, 16), :].astype(BF16)
        return c

    lax.fori_loop(0, HALO // 16, narrow, 0)

    pl.semaphore_wait(barrier, 2 + line - 1 + n_x - 1 + 2 * (n_tp - 1))

    send_tail = pltpu.make_async_remote_copy(
        src_ref=x_ref.at[:, pl.ds(rows - XH, XH), :],
        dst_ref=tail,
        send_sem=halo_send.at[0],
        recv_sem=halo_recv.at[0],
        device_id={"ctx": nxt},
        device_id_type=MESH,
    )
    send_gate = pltpu.make_async_remote_copy(
        src_ref=gsend,
        dst_ref=ghalo,
        send_sem=halo_send.at[1],
        recv_sem=halo_recv.at[1],
        device_id={"ctx": nxt},
        device_id_type=MESH,
    )
    send_tail.start()
    send_gate.start()
    own_block.wait()
    serve(0)

    for load in loads[2:]:
        load.wait()
    for t in range(tiles):
        mt_s[t] = mtaps_ref[:, pl.ds(t * 128, 128)]

    rate = rate_ref[...]
    angle = angle_ref[...]
    mag = jnp.exp(-rate)
    pr = mag * jnp.cos(angle)
    pi = mag * jnp.sin(angle)
    amp = jnp.sqrt(1.0 - jnp.exp(-2.0 * rate))
    rr = res_ref[0] * amp
    ri = res_ref[1] * amp
    put(pr_s, pr)
    put(pi_s, pi)
    put(a1_s, 2.0 * pr)
    put(a2_s, -(pr * pr + pi * pi))
    put(rr_s, rr)
    put(ri_s, ri)
    put(b1_s, -(rr * pr + ri * pi))

    def square(z):
        return z[0] * z[0] - z[1] * z[1], 2.0 * z[0] * z[1]

    z4 = square(square((pr, pi)))
    z16 = square(square(z4))
    z20 = (z16[0] * z4[0] - z16[1] * z4[1], z16[0] * z4[1] + z16[1] * z4[0])
    z40 = square(z20)
    z80 = square(z40)
    z160 = square(z80)
    for (fr, fi), power in zip(
        ((p20r, p20i), (p40r, p40i), (p80r, p80i), (p160r, p160i)), (z20, z40, z80, z160)
    ):
        put(fr, power[0])
        put(fi, power[1])

    sub = lax.broadcasted_iota(jnp.int32, (SUB, 128), 0)
    bits = [lax.rem(sub, 2) == 1, lax.rem(sub // 2, 2) == 1, sub >= 4]
    past = [sub >= 1, sub >= 2, sub >= 4]

    def powers(m, c):
        def at(l, cc):
            zr = jnp.where(bits[0], row(p20r, m, l), 1.0)
            zi = jnp.where(bits[0], row(p20i, m, l), 0.0)
            for bit, (fr, fi) in zip(bits[1:], ((p40r, p40i), (p80r, p80i))):
                ar = jnp.where(bit, row(fr, m, l), 1.0)
                ai = jnp.where(bit, row(fi, m, l), 0.0)
                zr, zi = zr * ar - zi * ai, zr * ai + zi * ar
            to = pl.ds(pl.multiple_of(m * SUB, SUB), SUB)
            qr[to, lanes(l)] = zr
            qi[to, lanes(l)] = zi
            return cc

        return lax.fori_loop(0, tiles, at, c)

    lax.fori_loop(0, modes, powers, 0)

    serve(1)
    send_tail.wait_recv()
    for s in range(3):
        rim = jnp.where(me > 0, tail[s].astype(F32), 0.0)
        for t in range(tiles):
            xf[s * tiles + t, pl.ds(0, XH), :] = rim[:, t * 128 : (t + 1) * 128]

    def rim_rows(l, c):
        gates(l, 0, 6)
        queries(l, 0, span)
        return c

    lax.fori_loop(0, tiles, rim_rows, 0)

    serve(2)
    send_gate.wait_recv()
    serve(3)

    def rim_gates(i, c):
        at = pl.ds(pl.multiple_of(i * 16, 16), 16)
        rim = jnp.where(me > 0, ghalo[at, :].astype(F32), 0.0)
        for t in range(tiles):
            gext[t, at, :] = rim[:, t * 128 : (t + 1) * 128]
        return c

    lax.fori_loop(0, HALO // 16, rim_gates, 0)


    def first_send(j):
        return pltpu.make_async_remote_copy(
            src_ref=ebuf.at[pl.ds(j * each, each)],
            dst_ref=rbuf.at[spot],
            send_sem=s1,
            recv_sem=r1,
            device_id=on_line(j),
            device_id_type=MESH,
        )

    def tile(l, c):
        def taps8(jb, acc):
            base = HALO - jb * 8
            taps = [row(mt_s, jb * 8 + jj, l) for jj in range(8)]
            got = {
                d: gext[l, pl.ds(base + d, SUB, stride=span), :]
                for d in range(-7, span)
            }
            out = []
            for k in range(span):
                v = acc[k]
                for jj in range(8):
                    v = v + taps[jj] * got[k - jj]
                out.append(v)
            return tuple(out)

        zero = jnp.zeros((SUB, 128), F32)
        acc = lax.fori_loop(0, HALO // 8, taps8, (zero,) * span)
        for k in range(span):
            med[pl.ds(k * SUB, SUB), lanes(l)] = acc[k]
        serve_in(l, 4, 8)

        def ends(g, cc):
            ms = [g * GROUP + i for i in range(GROUP)]
            a1 = [row(a1_s, m, l) for m in ms]
            a2 = [row(a2_s, m, l) for m in ms]
            w1 = [zero] * GROUP
            w2 = [zero] * GROUP
            for k in range(span):
                x = med[pl.ds(k * SUB, SUB), lanes(l)]
                w = [x + a1[i] * w1[i] + a2[i] * w2[i] for i in range(GROUP)]
                w2 = w1
                w1 = w
            q = l * groups + g
            for i, m in enumerate(ms):
                er = w1[i] - row(pr_s, m, l) * w2[i]
                ei = row(pi_s, m, l) * w2[i]
                to = pl.ds(pl.multiple_of(m * SUB, SUB), SUB)
                xr[to, lanes(l)] = er
                xi[to, lanes(l)] = ei
                for d, (fr, fi) in zip(
                    (1, 2, 4), ((p20r, p20i), (p40r, p40i), (p80r, p80i))
                ):
                    br = pltpu.roll(er, d, 0)
                    bi = pltpu.roll(ei, d, 0)
                    ar = row(fr, m, l)
                    ai = row(fi, m, l)
                    er, ei = er + ar * br - ai * bi, ei + ar * bi + ai * br
                ebuf[q, pl.ds(i, 1), :] = er[SUB - 1 :, :]
                ebuf[q, pl.ds(GROUP + i, 1), :] = ei[SUB - 1 :, :]
            return cc

        lax.fori_loop(0, groups, ends, c)
        for j in range(l * groups // each, (l + 1) * groups // each):

            @pl.when(spot != j)
            def _(j=j):
                first_send(j).start()

            @pl.when(spot == j)
            def _(j=j):
                rbuf[spot] = ebuf[pl.ds(j * each, each)]

        return c

    for l in range(tiles):
        tile(l, 0)
    for k in range(4 + tiles, 12):
        serve(k)

    serve(12)

    def local(l, c):
        def part(g, acc):
            out = list(acc)
            ms = [g * GROUP + i for i in range(GROUP)]
            a1 = [row(a1_s, m, l) for m in ms]
            a2 = [row(a2_s, m, l) for m in ms]
            b0 = [row(rr_s, m, l) for m in ms]
            b1 = [row(b1_s, m, l) for m in ms]
            zero = jnp.zeros((SUB, 128), F32)
            w1 = [zero] * GROUP
            w2 = [zero] * GROUP
            for k in range(span):
                x = med[pl.ds(k * SUB, SUB), lanes(l)]
                w = [x + a1[i] * w1[i] + a2[i] * w2[i] for i in range(GROUP)]
                for i in range(GROUP):
                    out[k] = out[k] + (b0[i] * w[i] + b1[i] * w1[i])
                w2 = w1
                w1 = w
            return tuple(out)

        skip = fixed_row(skip_ref, 0, l)
        acc = tuple(skip * med[pl.ds(k * SUB, SUB), lanes(l)] for k in range(span))
        acc = lax.fori_loop(0, groups, part, acc)
        for k in range(span):
            loc[pl.ds(k * SUB, SUB), lanes(l)] = acc[k]
        if l == min(3, tiles - 1):
            serve(13)
        return c

    for l in range(tiles):
        local(l, 0)
    serve(14)

    def await_tiles(ref, count, sem):
        some = ref.at[pl.ds(0, count)]
        pltpu.make_async_copy(some, some, sem).wait()

    def total_send(dx):
        return pltpu.make_async_remote_copy(
            src_ref=tot.at[x],
            dst_ref=tot.at[x],
            send_sem=t_send.at[dx],
            recv_sem=t_recv.at[dx],
            device_id=device(at_x(dx), z),
            device_id_type=MESH,
        )

    def reply(i):
        return pltpu.make_async_remote_copy(
            src_ref=obuf.at[i],
            dst_ref=sbuf.at[pl.ds(spot * each, each)],
            send_sem=s2,
            recv_sem=r2,
            device_id=on_line(i),
            device_id_type=MESH,
        )

    await_tiles(rbuf, line - 1, r1)

    def turn(q):
        l = q // groups
        g = lax.rem(q, groups)
        dr = jnp.zeros((SUB, 128), F32)
        di = jnp.zeros((SUB, 128), F32)
        for i in range(GROUP):
            here = lax.rem(sub, GROUP) == i
            dr = jnp.where(here, row(p160r, g * GROUP + i, l), dr)
            di = jnp.where(here, row(p160i, g * GROUP + i, l), di)
        return dr, jnp.where(sub < GROUP, -di, di)

    def turned(by, st):
        return by[0] * st + by[1] * pltpu.roll(st, GROUP, 0)

    zero = jnp.zeros((SUB, 128), F32)
    by = [turn(spot * each + u) for u in range(each)]
    states = [zero] * each
    for i in range(line):
        states = [turned(by[u], states[u]) + rbuf[i, u] for u in range(each)]
    for u in range(each):
        tot[x, u] = states[u]
    for dx in range(1, n_x):
        total_send(dx).start()
    serve(15)
    far = by
    for _ in range(line.bit_length() - 1):
        far = [(a * a - b * b, 2.0 * a * b) for a, b in far]
    for dx in range(1, n_x):
        total_send(dx).wait_recv()
    states = [zero] * each
    for xx in range(n_x):
        states = [
            jnp.where(xx < x, turned(far[u], states[u]) + tot[xx, u], states[u])
            for u in range(each)
        ]
    for i in range(line):
        for u in range(each):
            obuf[i, u] = states[u]
        if i < line - 1:
            states = [turned(by[u], states[u]) + rbuf[i, u] for u in range(each)]

    def answer(r, c):
        reply(lax.rem(spot + r, line)).start()
        return c

    lax.fori_loop(1, line, answer, 0)
    sbuf[pl.ds(spot * each, each)] = obuf[spot]

    serve(16)
    def before(g, c):
        for l in range(tiles):
            for i in range(GROUP):
                m = g * GROUP + i
                at = pl.ds(pl.multiple_of(m * SUB, SUB), SUB)
                er = jnp.where(past[0], pltpu.roll(xr[at, lanes(l)], 1, 0), 0.0)
                ei = jnp.where(past[0], pltpu.roll(xi[at, lanes(l)], 1, 0), 0.0)
                for d, keep, (fr, fi) in zip(
                    (1, 2, 4), past, ((p20r, p20i), (p40r, p40i), (p80r, p80i))
                ):
                    br = jnp.where(keep, pltpu.roll(er, d, 0), 0.0)
                    bi = jnp.where(keep, pltpu.roll(ei, d, 0), 0.0)
                    ar = row(fr, m, l)
                    ai = row(fi, m, l)
                    er, ei = er + ar * br - ai * bi, ei + ar * bi + ai * br
                xr[at, lanes(l)] = er
                xi[at, lanes(l)] = ei
        return c

    lax.fori_loop(0, groups, before, 0)
    serve(20)
    await_tiles(sbuf, (line - 1) * each, r2)

    def finish(l, c):
        def part(g, acc):
            out = list(acc)
            q = l * groups + g
            for i in range(GROUP):
                m = g * GROUP + i
                inr = jnp.broadcast_to(sbuf[q, pl.ds(i, 1), :], (SUB, 128))
                ini = jnp.broadcast_to(sbuf[q, pl.ds(GROUP + i, 1), :], (SUB, 128))
                at = pl.ds(pl.multiple_of(m * SUB, SUB), SUB)
                zr = qr[at, lanes(l)]
                zi = qi[at, lanes(l)]
                sr = xr[at, lanes(l)] + zr * inr - zi * ini
                si = xi[at, lanes(l)] + zr * ini + zi * inr
                rr = row(rr_s, m, l)
                ri = row(ri_s, m, l)
                ar = rr * sr - ri * si
                ai = rr * si + ri * sr
                u2 = ar
                u1 = ar * row(pr_s, m, l) - ai * row(pi_s, m, l)
                a1 = row(a1_s, m, l)
                a2 = row(a2_s, m, l)
                for k in range(span):
                    out[k] = out[k] + u1
                    u1, u2 = a1 * u1 + a2 * u2, u1
            return tuple(out)

        acc = tuple(loc[pl.ds(k * SUB, SUB), lanes(l)] for k in range(span))
        acc = lax.fori_loop(0, groups, part, acc)
        for k in range(span):
            hid = qs[pl.ds(k * SUB, SUB), lanes(l)] * acc[k]
            hid32[l, pl.ds(k, SUB, stride=span), :] = hid
        h2[core, :, lanes(l)] = hid32[l].astype(BF16)
        send_hidden(l).start()
        if l == min(4, tiles - 1):
            serve(17)
        return c

    def send_hidden(l):
        return pltpu.make_async_remote_copy(
            src_ref=h2.at[core, :, lanes(l)],
            dst_ref=h2.at[core, :, lanes(l)],
            send_sem=h_send,
            recv_sem=h_recv,
            device_id={"ctx": other},
            device_id_type=MESH,
        )

    for l in range(tiles):
        finish(l, 0)

    pltpu.make_async_copy(h2.at[1 - core], h2.at[1 - core], h_recv).wait()

    both = h2[...].reshape(2 * rows, width)
    sets = [order[:4], order[4:6], order[6:]] if n_z == 8 else [order]

    def used(g):
        return pl.ds(0, wide * len(sets[g]))

    def columns(g, r):
        to = lax.rem(tp + r, n_tp)
        w = jnp.concatenate([wt[to * n_z + at_z(dz)] for dz in sets[g]], 0)
        return lax.dot_general(both, w, (((1,), (1,)), ((), ())), preferred_element_type=F32)

    def to_y(g, r, cc):
        return pltpu.make_async_remote_copy(
            src_ref=snd.at[g, r - 1, cc, :, used(g)],
            dst_ref=rcv.at[g, r - 1, core, :, used(g)],
            send_sem=y_send.at[g, r - 1, cc],
            recv_sem=y_recv.at[g, r - 1, core],
            device_id={"ctx": me - core + cc, "tp": lax.rem(tp + r, n_tp)},
            device_id_type=MESH,
        )

    def via(g, cc):
        return pltpu.make_async_remote_copy(
            src_ref=snd.at[g, 1, cc, :, used(g)],
            dst_ref=rel.at[g, cc, :, used(g)],
            send_sem=y_send.at[g, 1, cc],
            recv_sem=v_recv.at[g, cc],
            device_id={"tp": lax.rem(tp + (1 if cc == 0 else n_tp - 1), n_tp)},
            device_id_type=MESH,
        )

    def to_core(g):
        return pltpu.make_async_remote_copy(
            src_ref=part.at[g, 1 - core, :, used(g)],
            dst_ref=rcvp.at[g, :, used(g)],
            send_sem=c_send.at[g],
            recv_sem=c_recv.at[g],
            device_id={"ctx": other},
            device_id_type=MESH,
        )

    ring = n_tp == 4
    near = (1, 3) if ring else tuple(range(1, n_tp))
    held = ((1, 0), (3, 1)) if ring else ()

    def project(g, between):
        if ring:
            got = columns(g, 2)
            for cc in range(2):
                snd[g, 1, cc, :, used(g)] = got[cc * rows : (cc + 1) * rows].astype(BF16)
                via(g, cc).start()
        for r in near:
            got = columns(g, r)
            for cc in range(2):
                block = got[cc * rows : (cc + 1) * rows]
                if (r, cc) in held:
                    hold[g, cc, :, used(g)] = block
                else:
                    snd[g, r - 1, cc, :, used(g)] = block.astype(BF16)
                    to_y(g, r, cc).start()
            if between:
                serve(between.pop(0))
        got = columns(g, 0)
        for cc in range(2):
            part[g, cc, :, used(g)] = got[cc * rows : (cc + 1) * rows]
        to_core(g).start()
        while between:
            serve(between.pop(0))

    def hand_over(g):
        for r, cc in held:
            via(g, cc).wait_recv()
            snd[g, r - 1, cc, :, used(g)] = (
                hold[g, cc, :, used(g)] + rel[g, cc, :, used(g)].astype(F32)
            ).astype(BF16)
            to_y(g, r, cc).start()

    def collect(g):
        to_core(g).wait_recv()
        for r in near:
            for cc in range(2):
                block = rcv.at[g, r - 1, cc, :, used(g)]
                pltpu.make_async_copy(block, block, y_recv.at[g, r - 1, cc]).wait()

        def add(i, c):
            at = pl.ds(pl.multiple_of(i * 32, 32), 32)
            mine_sum = part[g, core, at, used(g)]
            other_sum = rcvp[g, at, used(g)]
            for r in near:
                mine_sum = mine_sum + rcv[g, r - 1, core, at, used(g)].astype(F32)
                other_sum = other_sum + rcv[g, r - 1, 1 - core, at, used(g)].astype(F32)
            a = jnp.where(core == 0, mine_sum, other_sum)
            b = jnp.where(core == 0, other_sum, mine_sum)
            low = lax.broadcasted_iota(jnp.int32, (32, 128), 1) < wide
            for t in range(len(sets[g]) // 2):
                at_t = slice(t * 128, (t + 1) * 128)
                ones = (
                    jnp.where(low, a[:, at_t], pltpu.roll(b[:, at_t], wide, 1)),
                    jnp.where(low, pltpu.roll(a[:, at_t], wide, 1), b[:, at_t]),
                )
                for dz, one in zip(sets[g][2 * t : 2 * t + 2], ones):
                    to = pl.multiple_of(at_z(dz) * 2 * wide, 128)
                    out_ref[at, pl.ds(to, 2 * wide)] = one.astype(BF16)
            return c

        lax.fori_loop(0, rows // 32, add, 0)

    def need_set(g):
        for half_ in range(2):
            for dx in dxs:
                for dz in sets[g]:
                    need(half_, dx, dz)

    last = len(sets) - 1
    need_set(0)
    project(0, [18])
    serve(19)
    hand_over(0)
    for g in range(1, last + 1):
        need_set(g)
        project(g, [])
    for g in range(1, last + 1):
        hand_over(g)
    for g in range(last + 1):
        collect(g)

    for what in sends:
        pass_on(*what).wait_send()
    pltpu.make_async_copy(h2.at[core], h2.at[core], h_send).wait()
    for g in range(len(sets)):
        to_core(g).wait_send()
        for cc in range(2):
            if ring:
                via(g, cc).wait_send()
            for r in near:
                to_y(g, r, cc).wait_send()

    send_tail.wait_send()
    send_gate.wait_send()

    await_tiles(ebuf, (line - 1) * each, s1)
    await_tiles(obuf, line - 1, s2)
    for dx in range(1, n_x):
        total_send(dx).wait_send()


def vmem(shape, dtype=F32):
    return pltpu.VMEM(shape, dtype)


def body(n_ctx, n_tp, streams, short_taps, mix_taps, pole_rate, pole_angle, residue, skip, out_weight):
    rows, three, width = streams.shape
    modes = pole_rate.shape[0]
    tiles = width // 128
    total = (modes // GROUP) * tiles
    cols = out_weight.shape[1]
    line = n_ctx // n_tp
    deep = n_ctx // (2 * n_tp)
    sets = 3 if deep == 8 else 1
    half = cols * (4 if deep == 8 else deep)
    coef = [vmem((tiles, modes, 128))] * 15
    vm = pl.BlockSpec(memory_space=pltpu.VMEM)
    hbm = pl.BlockSpec(memory_space=pl.ANY)
    return pl.pallas_call(
        functools.partial(block_kernel, n_ctx, n_tp),
        out_shape=jax.ShapeDtypeStruct((rows, 2 * deep * cols), BF16),
        in_specs=[hbm] * 8,
        out_specs=vm,
        scratch_shapes=[
            vmem((3, rows, width), BF16),
            vmem((3, 7, width)),
            vmem((HALO, width)),
            vmem((modes, width)),
            vmem((modes, width)),
            vmem((2, modes, width)),
            vmem((1, width)),
            pltpu.SemaphoreType.DMA((7,)),
            vmem((3 * tiles, XH + rows, 128)),
            vmem((tiles, HALO + rows, 128)),
            vmem((HALO, width), BF16),
            vmem((HALO, width), BF16),
            vmem((3, XH, width), BF16),
            vmem((rows, width)),
            vmem((rows, width)),
            vmem((rows, width)),
            vmem((tiles, rows, 128)),
            vmem((modes * SUB, width)),
            vmem((modes * SUB, width)),
            vmem((modes * SUB, width)),
            vmem((modes * SUB, width)),
            *coef,
            vmem((tiles, HALO, 128)),
            vmem((total, 8, 128)),
            vmem((line, total // line, 8, 128)),
            vmem((line, total // line, 8, 128)),
            vmem((total, 8, 128)),
            vmem((n_tp, total // line, 8, 128)),
            pltpu.SemaphoreType.DMA((n_tp,)),
            pltpu.SemaphoreType.DMA((n_tp,)),
            pltpu.SemaphoreType.DMA((2,)),
            pltpu.SemaphoreType.DMA((2,)),
            pltpu.SemaphoreType.DMA,
            pltpu.SemaphoreType.DMA,
            pltpu.SemaphoreType.DMA,
            pltpu.SemaphoreType.DMA,
            vmem((n_ctx // 2, cols, width), BF16),
            vmem((2, rows, width), BF16),
            pltpu.SemaphoreType.DMA,
            pltpu.SemaphoreType.DMA((2 * n_ctx,)),
            pltpu.SemaphoreType.DMA((n_ctx,)),
            pltpu.SemaphoreType.DMA,
            pltpu.SemaphoreType.DMA,
            vmem((sets, 2, rows, half)),
            vmem((sets, n_tp - 1, 2, rows, half), BF16),
            vmem((sets, 2, rows, half), BF16),
            vmem((sets, n_tp - 1, 2, rows, half), BF16),
            vmem((sets, rows, half)),
            vmem((sets, 2, rows, half)),
            pltpu.SemaphoreType.DMA((sets, n_tp - 1, 2)),
            pltpu.SemaphoreType.DMA((sets, n_tp - 1, 2)),
            pltpu.SemaphoreType.DMA((sets, 2)),
            pltpu.SemaphoreType.DMA((sets,)),
            pltpu.SemaphoreType.DMA((sets,)),
        ],
        compiler_params=pltpu.CompilerParams(collective_id=0, has_side_effects=True),
        name="hyena_block",
    )(
        streams.transpose(1, 0, 2),
        short_taps.transpose(1, 0, 2),
        mix_taps,
        pole_rate,
        pole_angle,
        residue,
        skip[None],
        out_weight.T,
    )


def solution(mesh):
    return jax.shard_map(
        functools.partial(body, mesh.shape["ctx"], mesh.shape["tp"]),
        mesh=mesh,
        in_specs=(
            P("ctx", None, "tp"),
            P(None, None, "tp"),
            P(None, "tp"),
            P(None, "tp"),
            P(None, "tp"),
            P(None, None, "tp"),
            P("tp"),
            P("tp", "ctx"),
        ),
        out_specs=P("ctx", "tp"),
        check_vma=False,
    )
```
